32 devices in a mesh: dp: 2 (over x), row: 8 (over z, y), col: 2 (over core).
Axes of the slice: x: 2, y: 2, z: 4, core: 2. Of those that a mesh axis runs over, the one named last changes fastest.
Arguments:
- layer_input: bfloat16 [2048, 2048], P(('dp', 'col'), 'row'), may hold values from -6 to 6
- mixer_gain: float32 [2048], P('row'), may hold values from 0.5 to 1.5
- mixer_bias: float32 [2048], P('row'), may hold values from -3 to 3
- query_weight: bfloat16 [2048, 2048], P('row', 'col'), may hold values from -0.125 to 0.125
- key_weight: bfloat16 [2048, 2048], P('row', 'col'), may hold values from -0.125 to 0.125
- value_weight: bfloat16 [2048, 4096], P('row', 'col'), may hold values from -0.125 to 0.125
- gate_weight: bfloat16 [2048, 4096], P('row', 'col'), may hold values from -0.125 to 0.125
- output_weight: bfloat16 [4096, 2048], P('col', 'row'), may hold values from -0.1875 to 0.1875
- feed_gain: float32 [2048], P('row'), may hold values from 0.5 to 1.5
- feed_bias: float32 [2048], P('row'), may hold values from -3 to 3
- feed_gate: bfloat16 [2048, 4096], P('row', 'col'), may hold values from -0.125 to 0.125
- feed_up: bfloat16 [2048, 4096], P('row', 'col'), may hold values from -0.125 to 0.125
- feed_down: bfloat16 [4096, 2048], P('col', 'row'), may hold values from -0.1875 to 0.1875
- segments: int32 [2048], P(('dp', 'row')), may hold values from 0 to 1, never falling along the last dimension, each value on 1 to 2000 neighbouring positions
- upstream: bfloat16 [2048, 2048], P(('dp', 'col'), 'row'), may hold values from -6 to 6
Outputs:
- layer_output: bfloat16 [2048, 2048], P(('dp', 'col'), 'row')
- delta_input: float32 [2048, 2048], P(('dp', 'col'), 'row')
- delta_mixer_gain: float32 [2048], P('row')
- delta_mixer_bias: float32 [2048], P('row')
- delta_query_weight: float32 [2048, 2048], P('row', 'col')
- delta_key_weight: float32 [2048, 2048], P('row', 'col')
- delta_value_weight: float32 [2048, 4096], P('row', 'col')
- delta_gate_weight: float32 [2048, 4096], P('row', 'col')
- delta_output_weight: float32 [4096, 2048], P('col', 'row')
- delta_feed_gain: float32 [2048], P('row')
- delta_feed_bias: float32 [2048], P('row')
- delta_feed_gate: float32 [2048, 4096], P('row', 'col')
- delta_feed_up: float32 [2048, 4096], P('row', 'col')
- delta_feed_down: float32 [4096, 2048], P('col', 'row')
The draws below stay inside these ranges and needn't reach their ends.
Inputs may be any that keep to these rules, and one draw needn't show every extreme that they name: `segments`: document numbers never fall along the tokens; each document holds 1 to 2000 tokens.
All inputs are finite; a program needn't handle non-finite values.
Results may differ from the reference program's by a relative error of at most 0.011.
The reference program's roundings to bfloat16 on the way (of `mixer_in`, `hidden`, `feed_in`, `middle` and `delta_gate`) count: a program that leaves them out, or rounds other values in their place, can miss the bound.
Values may be sent and summed in bfloat16 or wider, within the bound.
No kernel may reach another device: no remote copies, remote signals or barrier semaphores. Data moves between devices by JAX's collectives and lax.ppermute only.
A program may use at most 192 MiB of HBM per device.

```python
import math
import jax
import jax.numpy as jnp
import numpy as np
from jax import lax

D = 2048
DK = 2048
DV = 4096
FF = 4096
HEADS = 8
TOK_DEV = 128
DOC_MAX = 2000
HK = 256
HV = 512
LENGTH = 1024
TOKENS = 2048
DOCS = 2
N_DP = 2
N_ROW = 8


def steps_of(key, extent, split, low, top_value):
    loudness, own = 1.0, jax.random.fold_in(key, 6)
    for dim, parts in split:
        draws = jnp.exp(jax.random.uniform(jax.random.fold_in(own, dim), (parts,), jnp.float32, low / len(split), top_value / len(split)))
        loudness = loudness * jnp.repeat(draws, extent[dim] // parts).reshape([-1 if axis == dim else 1 for axis in range(len(extent))])
    return loudness


def length_profile(number_of, total, limit, skew):
    weights = [(1 << 20) // math.isqrt(grade ** skew) + 1 for grade in range(2, number_of + 1)]
    surplus, holding = total - limit - (number_of - 1), [1] * (number_of - 1)
    while surplus > 0:
        candidates = [i for i in range(number_of - 1) if holding[i] < limit]
        pool, left = sum([weights[i] for i in candidates]), surplus
        for i in candidates:
            addition = min(limit - holding[i], max(1, left * weights[i] // pool), surplus)
            holding[i] = holding[i] + addition
            surplus = surplus - addition
    return np.array([limit] + holding)


def uneven(rng, count, total, reach, slope):
    if count == 2:
        one = jax.random.randint(rng, (), max(1, total - reach), min(reach, total - 1) + 1)
        return jnp.stack([one, total - one])
    tallies = jnp.asarray(length_profile(count, total, reach, slope), jnp.int32)
    couples = (count - 1) // 2
    giver, sink = tallies[1:1 + 2 * couples:2], tallies[2:2 + 2 * couples:2]
    slack = jnp.minimum(giver - 1, reach - sink)
    passed = jax.random.randint(jax.random.fold_in(rng, 1), (couples,), 0, 1 << 20) % (slack + 1)
    tallies = tallies.at[1:1 + 2 * couples:2].set(giver - passed).at[2:2 + 2 * couples:2].set(sink + passed)
    return tallies[jax.random.permutation(jax.random.fold_in(rng, 2), count)]


def gaussian(own_key, shape, deviation, bound, cuts=(), held_as=jnp.bfloat16):
    level = steps_of(own_key, shape, cuts, -0.22, 0.18) if cuts else 1.0
    drawn = jax.random.normal(own_key, shape, jnp.float32) * deviation * level
    return jnp.minimum(jnp.maximum(drawn, -bound), bound).astype(held_as)


def setup_inputs(seed: int = 0) -> dict:
    splits = jax.random.split(jax.random.key(seed), 16)
    layer_input = gaussian(splits[0], (TOKENS, D), 1.0, 6.0, ((0, 4), (1, 8)))
    mixer_gain = jnp.clip(1.0 + 0.1 * jax.random.normal(splits[1], (D,), jnp.float32), 0.5, 1.5)
    mixer_bias = gaussian(splits[2], (D,), 0.5, 3.0, ((0, 8),), jnp.float32)
    query_weight = gaussian(splits[3], (D, DK), D ** -0.5, 0.125, ((0, 8), (1, 2)))
    key_weight = gaussian(splits[4], (D, DK), D ** -0.5, 0.125, ((0, 8), (1, 2)))
    value_weight = gaussian(splits[5], (D, DV), D ** -0.5, 0.125, ((0, 8), (1, 2)))
    gate_weight = gaussian(splits[6], (D, DV), D ** -0.5, 0.125, ((0, 8), (1, 2)))
    output_weight = gaussian(splits[7], (DV, D), (DV // 4) ** -0.5, 0.1875, ((0, 2), (1, 8)))
    feed_gain = jnp.clip(1.0 + 0.1 * jax.random.normal(splits[8], (D,), jnp.float32), 0.5, 1.5)
    feed_bias = gaussian(splits[9], (D,), 0.5, 3.0, ((0, 8),), jnp.float32)
    feed_gate = gaussian(splits[10], (D, FF), D ** -0.5, 0.125, ((0, 8), (1, 2)))
    feed_up = gaussian(splits[11], (D, FF), D ** -0.5, 0.125, ((0, 8), (1, 2)))
    feed_down = gaussian(splits[12], (FF, D), (FF // 4) ** -0.5, 0.1875, ((0, 2), (1, 8)))
    segments = jnp.searchsorted(jnp.cumsum(uneven(splits[13], DOCS, TOKENS, DOC_MAX, 2)), jnp.arange(TOKENS), side="right").astype(jnp.int32)
    upstream = gaussian(splits[14], (TOKENS, D), 1.0, 6.0, ((0, 4), (1, 8)))
    return dict(layer_input=layer_input, mixer_gain=mixer_gain, mixer_bias=mixer_bias, query_weight=query_weight, key_weight=key_weight, value_weight=value_weight, gate_weight=gate_weight, output_weight=output_weight, feed_gain=feed_gain, feed_bias=feed_bias, feed_gate=feed_gate, feed_up=feed_up, feed_down=feed_down, segments=segments, upstream=upstream)


NORM_EPS = 1e-05
EXACT_PRECISION = lax.Precision.HIGHEST

def decay_tables(segment_ids, log_gamma):
    length_here = segment_ids.shape[0]
    position = jnp.arange(length_here, dtype=jnp.float32)
    same_doc = segment_ids[:, None] == segment_ids[None, :]
    causal = position[:, None] >= position[None, :]
    distance = jnp.where(causal, position[:, None] - position[None, :], 0.0)
    decay_mask = jnp.where((same_doc & causal)[None], jnp.exp(log_gamma[:, None, None] * distance[None]), 0.0)
    leading = (segment_ids == segment_ids[0]).astype(jnp.float32)
    trailing = (segment_ids == segment_ids[-1]).astype(jnp.float32)
    incoming_state = jnp.exp(log_gamma[:, None] * (position + 1.0)[None]) * leading[None]
    outgoing_state = jnp.exp(log_gamma[:, None] * (length_here - 1.0 - position)[None]) * trailing[None]
    through = jnp.exp(log_gamma * length_here) * (segment_ids[0] == segment_ids[-1]).astype(jnp.float32)
    return (decay_mask, incoming_state, outgoing_state, through)

def local_retention(heads_of_query, heads_of_key, heads_of_value, decay_lookup):
    scores = jnp.einsum('htk,hsk->hts', heads_of_query, heads_of_key, precision=EXACT_PRECISION) * decay_lookup[0]
    local_out = jnp.einsum('hts,hsv->htv', scores, heads_of_value, precision=EXACT_PRECISION)
    within_segment_state = jnp.einsum('aji,ajy->aiy', heads_of_key * decay_lookup[2][:, :, None], heads_of_value, precision=EXACT_PRECISION)
    return (local_out, within_segment_state)

def cross_term(heads_of_query, decay_lookup, carried_over):
    return decay_lookup[1][:, :, None] * jnp.einsum('dez,dzl->del', heads_of_query, carried_over, precision=EXACT_PRECISION)

def retention_grads(heads_of_query, heads_of_key, heads_of_value, decay_lookup, carried_over, retention_gradient, state_gradient):
    decay_mask, incoming_state, outgoing_state = (decay_lookup[0], decay_lookup[1], decay_lookup[2])
    scores = jnp.einsum('htk,hsk->hts', heads_of_query, heads_of_key, precision=EXACT_PRECISION) * decay_mask
    delta_scores = jnp.einsum('htv,hsv->hts', retention_gradient, heads_of_value, precision=EXACT_PRECISION) * decay_mask
    query_gradient = jnp.einsum('hts,hsk->htk', delta_scores, heads_of_key, precision=EXACT_PRECISION)
    query_gradient = query_gradient + incoming_state[:, :, None] * jnp.einsum('pqf,pgf->pqg', retention_gradient, carried_over, precision=EXACT_PRECISION)
    key_gradient = jnp.einsum('hts,htk->hsk', delta_scores, heads_of_query, precision=EXACT_PRECISION)
    key_gradient = key_gradient + outgoing_state[:, :, None] * jnp.einsum('xwa,xma->xwm', heads_of_value, state_gradient, precision=EXACT_PRECISION)
    value_gradient = jnp.einsum('hts,htv->hsv', scores, retention_gradient, precision=EXACT_PRECISION)
    value_gradient = value_gradient + outgoing_state[:, :, None] * jnp.einsum('ipt,itx->ipx', heads_of_key, state_gradient, precision=EXACT_PRECISION)
    return (query_gradient, key_gradient, value_gradient)

def carried_grad(heads_of_query, decay_lookup, retention_gradient):
    return jnp.einsum('uye,uyj->uej', heads_of_query, decay_lookup[1][:, :, None] * retention_gradient, precision=EXACT_PRECISION)

def group_norm(retained):
    mean_square = lax.optimization_barrier(jnp.mean(retained * retained, axis=-1))
    rscale = lax.rsqrt(jnp.maximum(mean_square, 1.0))
    active = (mean_square > 1.0).astype(jnp.float32)
    return (retained * rscale[..., None], rscale, active)

def layer_norm(values, gain, bias):
    average = lax.optimization_barrier(jnp.mean(values, axis=1, keepdims=True))
    centred = values - average
    variance = lax.optimization_barrier(jnp.mean(centred * centred, axis=1, keepdims=True))
    rscale = lax.rsqrt(variance + NORM_EPS)
    normed = centred * rscale
    return (normed, rscale, (normed * gain + bias).astype(jnp.bfloat16))

def norm_back(delta, normed, rscale, gain):
    scaled = delta * gain
    back = rscale * (scaled - lax.optimization_barrier(jnp.mean(scaled, axis=1, keepdims=True)) - normed * lax.optimization_barrier(jnp.mean(scaled * normed, axis=1, keepdims=True)))
    return (back, lax.optimization_barrier(jnp.sum(delta * normed, axis=0)), lax.optimization_barrier(jnp.sum(delta, axis=0)))

def matmul(left, right):
    return jnp.dot(left, right, preferred_element_type=jnp.float32)

def matmul_back(left, right):
    return lax.dot_general(left, right, (((1,), (1,)), ((), ())), preferred_element_type=jnp.float32)

def to_blocks(matrix, width):
    return matrix.astype(jnp.float32).reshape(N_ROW, TOK_DEV, HEADS, width).transpose(0, 2, 1, 3)

def from_blocks(tensor):
    return tensor.transpose(0, 2, 1, 3).reshape(LENGTH, -1)

def stream_layer(layer_input, segment_ids, upstream, weights):
    mixer_gain, mixer_bias, query_weight, key_weight, value_weight, gate_weight, output_weight, feed_gain, feed_bias, feed_gate, feed_up, feed_down = weights
    key_scale = HK ** (-0.5)
    inputs_wide = layer_input.astype(jnp.float32)
    mixer_hat, mixer_rscale, mixer_in = layer_norm(inputs_wide, mixer_gain, mixer_bias)
    query = matmul(mixer_in, query_weight).astype(jnp.bfloat16)
    key_rows = (matmul(mixer_in, key_weight) * key_scale).astype(jnp.bfloat16)
    value_rows = matmul(mixer_in, value_weight).astype(jnp.bfloat16)
    gate_pre = matmul(mixer_in, gate_weight)
    log_gamma = jnp.log1p(-jnp.exp2(-5.0 - jnp.arange(HEADS, dtype=jnp.float32)))
    query_blocks = to_blocks(query, HK)
    key_blocks = to_blocks(key_rows, HK)
    value_blocks = to_blocks(value_rows, HV)
    segment_blocks = segment_ids.reshape(N_ROW, TOK_DEV)

    def forward_block(carry, block):
        state_in, last_id = carry
        heads_of_query, heads_of_key, heads_of_value, segment_block = block
        decay_lookup = decay_tables(segment_block, log_gamma)
        local_out, within_segment_state = local_retention(heads_of_query, heads_of_key, heads_of_value, decay_lookup)
        passing = (last_id == segment_block[0].astype(jnp.float32)).astype(jnp.float32)
        carried_over = passing * state_in
        retained = local_out + cross_term(heads_of_query, decay_lookup, carried_over)
        new_state = within_segment_state + decay_lookup[3][:, None, None] * carried_over
        return ((new_state, segment_block[-1].astype(jnp.float32)), (retained, carried_over, passing))
    start_carry = (jnp.zeros((HEADS, HK, HV), jnp.float32), jnp.full((), -1.0, jnp.float32))
    final_carry, stacked = lax.scan(forward_block, start_carry, (query_blocks, key_blocks, value_blocks, segment_blocks))
    retained, carried_all, passing_all = stacked
    normed_heads, head_rscale, head_active = group_norm(retained)
    out_normed = from_blocks(normed_heads)
    gate_sig = jax.nn.sigmoid(gate_pre)
    swish = gate_pre * gate_sig
    hidden = (swish * out_normed).astype(jnp.bfloat16)
    residual = inputs_wide + matmul(hidden, output_weight)
    feed_hat, feed_rscale, feed_in = layer_norm(residual, feed_gain, feed_bias)
    pre_gate = matmul(feed_in, feed_gate)
    pre_up = matmul(feed_in, feed_up)
    up_sig = jax.nn.sigmoid(pre_gate)
    activated = pre_gate * up_sig
    middle = (activated * pre_up).astype(jnp.bfloat16)
    layer_output = (residual + matmul(middle, feed_down)).astype(jnp.bfloat16)
    delta_down = matmul(middle.T, upstream)
    delta_middle = matmul_back(upstream, feed_down)
    delta_pre_gate = (delta_middle * pre_up * up_sig * (1.0 + pre_gate * (1.0 - up_sig))).astype(jnp.bfloat16)
    delta_pre_up = (delta_middle * activated).astype(jnp.bfloat16)
    delta_feed_gate = matmul(feed_in.T, delta_pre_gate)
    delta_feed_up = matmul(feed_in.T, delta_pre_up)
    delta_feed_in = matmul_back(delta_pre_gate, feed_gate) + matmul_back(delta_pre_up, feed_up)
    delta_feed_hat, delta_feed_gain, delta_feed_bias = norm_back(delta_feed_in, feed_hat, feed_rscale, feed_gain)
    delta_residual = upstream.astype(jnp.float32) + delta_feed_hat
    residual_narrow = delta_residual.astype(jnp.bfloat16)
    delta_output = matmul(hidden.T, residual_narrow)
    delta_hidden = matmul_back(residual_narrow, output_weight)
    delta_gate = (delta_hidden * out_normed * gate_sig * (1.0 + gate_pre * (1.0 - gate_sig))).astype(jnp.bfloat16)
    delta_heads = (delta_hidden * swish).reshape(N_ROW, TOK_DEV, HEADS, HV).transpose(0, 2, 1, 3)
    delta_retained = head_rscale[..., None] * (delta_heads - head_active[..., None] * normed_heads * lax.optimization_barrier(jnp.mean(delta_heads * normed_heads, axis=-1, keepdims=True)))

    def backward_block(state_gradient, block):
        heads_of_query, heads_of_key, heads_of_value, segment_block, carried_over, passing, delta_block = block
        decay_lookup = decay_tables(segment_block, log_gamma)
        grads = retention_grads(heads_of_query, heads_of_key, heads_of_value, decay_lookup, carried_over, delta_block, state_gradient)
        growth = carried_grad(heads_of_query, decay_lookup, delta_block)
        return (passing * (growth + decay_lookup[3][:, None, None] * state_gradient), grads)
    final_state, block_grads = lax.scan(backward_block, jnp.zeros((HEADS, HK, HV), jnp.float32), (query_blocks, key_blocks, value_blocks, segment_blocks, carried_all, passing_all, delta_retained), reverse=True)
    query_gradient = from_blocks(block_grads[0]).astype(jnp.bfloat16)
    key_gradient = (from_blocks(block_grads[1]) * key_scale).astype(jnp.bfloat16)
    value_gradient = from_blocks(block_grads[2]).astype(jnp.bfloat16)
    delta_query_weight = matmul(mixer_in.T, query_gradient)
    delta_key_weight = matmul(mixer_in.T, key_gradient)
    delta_value_weight = matmul(mixer_in.T, value_gradient)
    delta_gate_weight = matmul(mixer_in.T, delta_gate)
    delta_mixer_in = matmul_back(query_gradient, query_weight) + matmul_back(key_gradient, key_weight) + matmul_back(value_gradient, value_weight) + matmul_back(delta_gate, gate_weight)
    delta_mixer_hat, delta_mixer_gain, delta_mixer_bias = norm_back(delta_mixer_in, mixer_hat, mixer_rscale, mixer_gain)
    delta_input = delta_residual + delta_mixer_hat
    grads_all = (delta_mixer_gain, delta_mixer_bias, delta_query_weight, delta_key_weight, delta_value_weight, delta_gate_weight, delta_output, delta_feed_gain, delta_feed_bias, delta_feed_gate, delta_feed_up, delta_down)
    return (layer_output, delta_input, grads_all)

def reference(layer_input, mixer_gain, mixer_bias, query_weight, key_weight, value_weight, gate_weight, output_weight, feed_gain, feed_bias, feed_gate, feed_up, feed_down, segments, upstream):
    weights = (mixer_gain, mixer_bias, query_weight, key_weight, value_weight, gate_weight, output_weight, feed_gain, feed_bias, feed_gate, feed_up, feed_down)
    start_grads = tuple((jnp.zeros(w.shape, jnp.float32) for w in weights))

    def one_stream(totals, stream):
        stream_input, stream_segments, stream_upstream = stream
        layer_output, delta_input, grads_all = stream_layer(stream_input, stream_segments, stream_upstream, weights)
        return (tuple((a + b for a, b in zip(totals, grads_all))), (layer_output, delta_input))
    totals, outputs = lax.scan(one_stream, start_grads, (layer_input.reshape(N_DP, LENGTH, D), segments.reshape(N_DP, LENGTH), upstream.reshape(N_DP, LENGTH, D)))
    layer_output = outputs[0].reshape(TOKENS, D)
    delta_input = outputs[1].reshape(TOKENS, D)
    return (layer_output, delta_input, totals[0], totals[1], totals[2], totals[3], totals[4], totals[5], totals[6], totals[7], totals[8], totals[9], totals[10], totals[11])
```

```python
import jax
import jax.numpy as jnp
import numpy as np
from jax import lax
from jax.sharding import PartitionSpec as P

D = 2048
HK = 256
HV = 512
NORM_EPS = 1e-05
F32 = jnp.float32
BF16 = jnp.bfloat16


def ring_order(count):
    depth = 4
    if count % depth or count == depth:
        return list(range(count))
    width = count // depth
    walk = [(z, 0) for z in range(depth)]
    for z in reversed(range(depth)):
        cells = range(1, width) if (depth - 1 - z) % 2 == 0 else reversed(range(1, width))
        walk += [(z, y) for y in cells]
    return [z * width + y for z, y in walk]


class Row:
    def __init__(self):
        self.size = size = lax.axis_size("row")
        self.order = order = ring_order(size)
        where = [order.index(i) for i in range(size)]
        me = lax.axis_index("row")
        ahead = np.array([[order[(where[i] + k) % size] for k in range(size)] for i in range(size)])
        slot = np.array([[(where[j] - where[i]) % size for j in range(size)] for i in range(size)])
        self.me = me
        ahead_here = jnp.asarray(ahead, jnp.int32)[me]
        slot_here = jnp.asarray(slot, jnp.int32)[me]
        self.ahead = [ahead_here[k] for k in range(size)]
        self.slot = [slot_here[j] for j in range(size)]

    def send(self, value, shift):
        size, order = self.size, self.order
        return lax.ppermute(
            value, "row", [(order[i], order[(i + shift) % size]) for i in range(size)]
        )

    def gather(self, tile):
        size, half = self.size, self.size // 2
        slots = [None] * size
        slots[0] = forth = back = tile
        for step in range(1, half):
            forth = self.send(forth, 1)
            back = self.send(back, -1)
            slots[-step] = forth
            slots[step] = back
        cut = tile.shape[0] // 2
        slots[half] = jnp.concatenate([self.send(forth[:cut], 1), self.send(back[cut:], -1)], 0)
        return slots

    def scatter_sum(self, blocks):
        half = self.size // 2
        cut = blocks[0].shape[0] // 2
        far = blocks[half].astype(BF16)
        forth, back = far[:cut], far[cut:]
        forth = self.send(forth, 1)
        back = self.send(back, -1)
        for step in range(half - 1, 0, -1):
            ahead, behind = blocks[step].astype(F32), blocks[-step].astype(F32)
            if step == half - 1:
                ahead = jnp.concatenate([ahead[:cut] + forth.astype(F32), ahead[cut:]], 0)
                behind = jnp.concatenate([behind[:cut], behind[cut:] + back.astype(F32)], 0)
            else:
                ahead = ahead + forth.astype(F32)
                behind = behind + back.astype(F32)
            forth = self.send(ahead.astype(BF16), 1)
            back = self.send(behind.astype(BF16), -1)
        return blocks[0].astype(F32) + forth.astype(F32) + back.astype(F32)

    def exchange(self, blocks):
        got = [None] * self.size
        got[0] = blocks[0]
        for shift in range(1, self.size):
            got[-shift] = self.send(blocks[shift], shift)
        return got


def xor_send(value, axis, bit):
    size = lax.axis_size(axis)
    return lax.ppermute(value, axis, [(i, i ^ bit) for i in range(size)])


def xor_sum(value, axis, size):
    bit = 1
    while bit < size:
        value = value + xor_send(value, axis, bit)
        bit *= 2
    return value


def xor_gather(value, axis):
    me, size, bit = lax.axis_index(axis), lax.axis_size(axis), 1
    while bit < size:
        other = xor_send(value, axis, bit)
        upper = (me // bit) % 2 == 1
        value = jnp.concatenate(
            [jnp.where(upper, other, value), jnp.where(upper, value, other)], 0
        )
        bit *= 2
    return value


def product(left, right):
    return jnp.dot(left, right, preferred_element_type=F32)


def product_flipped(left, right):
    return lax.dot_general(left, right, (((1,), (1,)), ((), ())), preferred_element_type=F32)


def outer_sum(left, right):
    return lax.dot_general(left, right, (((0,), (0,)), ((), ())), preferred_element_type=F32)


def columns(matrix, index, width):
    return lax.dynamic_slice_in_dim(matrix, index * width, width, 1)


def rows(matrix, index, width):
    return lax.dynamic_slice_in_dim(matrix, index * width, width, 0)


def sum_cols(partial):
    size, mine = lax.axis_size("col"), lax.axis_index("col")
    count = partial.shape[0] // size
    total = rows(partial, mine, count).astype(F32)
    for bit in range(1, size):
        total = total + xor_send(rows(partial, mine ^ bit, count).astype(BF16), "col", bit).astype(
            F32
        )
    return total


def swish_parts(pre):
    sig = jax.nn.sigmoid(pre)
    return pre * sig, sig * (1.0 + pre * (1.0 - sig))


def per_device(
    layer_input,
    mixer_gain,
    mixer_bias,
    query_weight,
    key_weight,
    value_weight,
    gate_weight,
    output_weight,
    feed_gain,
    feed_bias,
    feed_gate,
    feed_up,
    feed_down,
    segments,
    upstream,
):
    row = Row()
    size = row.size
    col_size, col = lax.axis_size("col"), lax.axis_index("col")
    key_scale = HK ** (-0.5)
    wq = query_weight.shape[1] // size
    wv = value_weight.shape[1] // size
    wf = feed_gate.shape[1] // size
    heads_here = query_weight.shape[1] // HK
    group = size // heads_here
    head = (col * heads_here + row.me // group).astype(F32)
    log_gamma = jnp.log1p(-jnp.exp2(-5.0 - head))
    tokens = layer_input.shape[0]
    length = tokens * col_size

    small = jnp.concatenate([segments.astype(F32), mixer_gain, mixer_bias])[None]
    small = xor_gather(small, "row")
    count = segments.shape[0]
    seg = small[:, :count].reshape(-1)
    gains = jnp.concatenate([rows(small, i, 1) for i in row.ahead], 0)
    gain_all = gains[:, count : count + mixer_gain.shape[0]].reshape(1, -1)
    bias_all = gains[:, count + mixer_gain.shape[0] :].reshape(1, -1)

    x_all = jnp.concatenate(row.gather(layer_input), 1).astype(F32)
    average = jnp.mean(x_all, axis=1, keepdims=True)
    centred = x_all - average
    mixer_rscale = lax.rsqrt(jnp.mean(centred * centred, axis=1, keepdims=True) + NORM_EPS)
    mixer_own = (centred * mixer_rscale * gain_all + bias_all).astype(BF16)
    mixer_in = xor_gather(mixer_own, "col")
    inputs_wide = layer_input.astype(F32)
    mixer_hat = (inputs_wide - average) * mixer_rscale

    w_qkv = row.exchange(
        [
            jnp.concatenate(
                [
                    columns(query_weight, i, wq),
                    columns(key_weight, i, wq),
                    columns(value_weight, i, wv),
                ],
                1,
            )
            for i in row.ahead
        ]
    )
    w_qkv = jnp.concatenate(w_qkv, 0)
    w_gate = jnp.concatenate(row.exchange([columns(gate_weight, i, wv) for i in row.ahead]), 0)
    out_rel = jnp.concatenate([rows(output_weight, i, wv) for i in row.ahead], 0)
    down_rel = jnp.concatenate([rows(feed_down, i, wf) for i in row.ahead], 0)
    w_out = jnp.concatenate(
        row.exchange([out_rel[k * wv : (k + 1) * wv] for k in range(size)]), 1
    )
    w_feed = row.exchange(
        [jnp.concatenate([columns(feed_gate, i, wf), columns(feed_up, i, wf)], 1) for i in row.ahead]
    )
    w_feed = jnp.concatenate(w_feed, 0)

    qkv = product(mixer_in, w_qkv)
    query_key = jnp.stack([qkv[:, :wq], qkv[:, wq : 2 * wq] * key_scale]).astype(BF16)
    value = qkv[:, 2 * wq :].astype(BF16)
    bit = 1
    while bit < group:
        query_key = jnp.concatenate([query_key, xor_send(query_key, "row", bit)], 2)
        bit *= 2
    query, key = query_key[0], query_key[1]
    place = jnp.arange(length, dtype=F32)
    distance = place[:, None] - place[None, :]
    admitted = (distance >= 0.0) & (seg[:, None] == seg[None, :])
    decay = jnp.where(admitted, jnp.exp(log_gamma * jnp.maximum(distance, 0.0)), 0.0)
    scores = (product_flipped(query, key) * decay).astype(BF16)
    retained = product(scores, value)
    square = xor_sum(jnp.sum(retained * retained, axis=1), "row", group) / HV
    head_rscale = lax.rsqrt(jnp.maximum(square, 1.0))[:, None]
    head_active = (square > 1.0).astype(F32)[:, None]
    out_normed = retained * head_rscale
    gate_pre = product(mixer_in, w_gate)
    swish, swish_slope = swish_parts(gate_pre)
    hidden = (swish * out_normed).astype(BF16)
    hidden_rel = jnp.concatenate(row.gather(hidden), 1)
    residual = inputs_wide + sum_cols_exact(product(hidden_rel, out_rel))

    sums = jnp.stack([jnp.sum(residual, axis=1), jnp.sum(residual * residual, axis=1)])
    sums = xor_sum(sums, "row", size) / D
    average = sums[0][:, None]
    feed_rscale = lax.rsqrt(sums[1][:, None] - average * average + NORM_EPS)
    feed_hat = (residual - average) * feed_rscale
    feed_own = (feed_hat * feed_gain + feed_bias).astype(BF16)
    feed_in = xor_gather(jnp.concatenate(row.gather(feed_own), 1), "col")
    feed_pre = product(feed_in, w_feed)
    pre_gate, pre_up = feed_pre[:, :wf], feed_pre[:, wf:]
    activated, activated_slope = swish_parts(pre_gate)
    middle = (activated * pre_up).astype(BF16)
    middle_rel = jnp.concatenate(row.gather(middle), 1)
    layer_output = (residual + sum_cols_exact(product(middle_rel, down_rel))).astype(BF16)

    upstream_all = xor_gather(upstream, "col")
    delta_middle_parts = product_flipped(upstream_all, down_rel)
    delta_middle = row.scatter_sum([delta_middle_parts[:, k * wf : (k + 1) * wf] for k in range(size)])
    delta_down = outer_sum(middle_rel, upstream_all)
    delta_pre = jnp.concatenate(
        [delta_middle * pre_up * activated_slope, delta_middle * activated], 1
    ).astype(BF16)
    wide = feed_gain.shape[0]
    delta_feed_parts = sum_cols(product_flipped(delta_pre, w_feed))
    delta_feed_in = row.scatter_sum([delta_feed_parts[:, k * wide : (k + 1) * wide] for k in range(size)])
    delta_feed_matrix = outer_sum(feed_in, delta_pre).astype(BF16)
    delta_feed_matrix = row.exchange([delta_feed_matrix[k * wide : (k + 1) * wide] for k in range(size)])

    scaled = delta_feed_in * feed_gain
    sums = jnp.stack([jnp.sum(scaled, axis=1), jnp.sum(scaled * feed_hat, axis=1)])
    sums = xor_sum(sums, "row", size) / D
    delta_residual = upstream.astype(F32) + feed_rscale * (
        scaled - sums[0][:, None] - feed_hat * sums[1][:, None]
    )
    delta_feed_gain = jnp.sum(delta_feed_in * feed_hat, axis=0)
    delta_feed_bias = jnp.sum(delta_feed_in, axis=0)

    narrow_own = delta_residual.astype(BF16)
    narrow_rel = xor_gather(jnp.concatenate(row.gather(narrow_own), 1), "col")
    delta_output = outer_sum(hidden_rel, narrow_rel[:, :wide])
    delta_hidden = product_flipped(narrow_rel, w_out)
    delta_gate = (delta_hidden * out_normed * swish_slope).astype(BF16)
    delta_normed = delta_hidden * swish
    mixed = xor_sum(jnp.sum(delta_normed * out_normed, axis=1), "row", group) / HV
    delta_retained = (
        head_rscale * (delta_normed - head_active * out_normed * mixed[:, None])
    ).astype(BF16)
    delta_scores = (product_flipped(delta_retained, value) * decay).astype(BF16)
    delta_query = product(delta_scores, key)
    delta_key = outer_sum(delta_scores, query)
    delta_value = outer_sum(scores, delta_retained)
    delta_qk = jnp.stack([delta_query, delta_key])
    bit = group // 2
    while bit >= 1:
        keep = delta_qk.shape[2] // 2
        delta_qk = delta_qk[:, :, :keep] + xor_send(
            delta_qk[:, :, keep:].astype(BF16), "row", bit
        ).astype(F32)
        bit //= 2
    delta_qkv = jnp.concatenate(
        [delta_qk[0], delta_qk[1] * key_scale, delta_value], 1
    ).astype(BF16)

    delta_mixer_parts = sum_cols(
        product_flipped(delta_qkv, w_qkv) + product_flipped(delta_gate, w_gate)
    )
    delta_mixer_in = row.scatter_sum(
        [delta_mixer_parts[:, k * wide : (k + 1) * wide] for k in range(size)]
    )
    scaled = delta_mixer_in * mixer_gain
    sums = jnp.stack([jnp.sum(scaled, axis=1), jnp.sum(scaled * mixer_hat, axis=1)])
    sums = xor_sum(sums, "row", size) / D
    delta_input = delta_residual + mixer_rscale * (
        scaled - sums[0][:, None] - mixer_hat * sums[1][:, None]
    )
    gains = jnp.stack(
        [
            jnp.sum(delta_mixer_in * mixer_hat, axis=0),
            jnp.sum(delta_mixer_in, axis=0),
            delta_feed_gain,
            delta_feed_bias,
        ]
    )
    gains = xor_sum(xor_sum(gains, "col", col_size), "dp", lax.axis_size("dp"))

    delta_qkv_matrix = outer_sum(mixer_in, delta_qkv).astype(BF16)
    delta_gate_matrix = outer_sum(mixer_in, delta_gate).astype(BF16)
    delta_qkv_matrix = row.exchange([delta_qkv_matrix[k * wide : (k + 1) * wide] for k in range(size)])
    delta_gate_matrix = row.exchange([delta_gate_matrix[k * wide : (k + 1) * wide] for k in range(size)])

    def over_dp(value):
        value = value.astype(BF16)
        total, bit = value.astype(F32), 1
        while bit < lax.axis_size("dp"):
            total = total + xor_send(value, "dp", bit).astype(F32)
            bit *= 2
        return total

    def placed(slots, *widths):
        total = over_dp(jnp.stack(slots))
        ordered = [lax.dynamic_index_in_dim(total, j, 0, False) for j in row.slot]
        outs, start = [], 0
        for width in widths:
            outs.append(jnp.concatenate([b[:, start : start + width] for b in ordered], 1))
            start += width
        return outs

    def placed_rows(matrix, width):
        total = over_dp(matrix)
        return jnp.concatenate([rows(total, j, width) for j in row.slot], 0)

    delta_query_weight, delta_key_weight, delta_value_weight = placed(delta_qkv_matrix, wq, wq, wv)
    (delta_gate_weight,) = placed(delta_gate_matrix, wv)
    delta_feed_gate, delta_feed_up = placed(delta_feed_matrix, wf, wf)
    return (
        layer_output,
        delta_input,
        gains[0],
        gains[1],
        delta_query_weight,
        delta_key_weight,
        delta_value_weight,
        delta_gate_weight,
        placed_rows(delta_output, wv),
        gains[2],
        gains[3],
        delta_feed_gate,
        delta_feed_up,
        placed_rows(delta_down, wf),
    )


def sum_cols_exact(partial):
    size, mine = lax.axis_size("col"), lax.axis_index("col")
    count = partial.shape[0] // size
    total = rows(partial, mine, count)
    for bit in range(1, size):
        total = total + xor_send(rows(partial, mine ^ bit, count), "col", bit)
    return total


def solution(mesh):
    in_specs = (
        P(("dp", "col"), "row"),
        P("row"),
        P("row"),
        P("row", "col"),
        P("row", "col"),
        P("row", "col"),
        P("row", "col"),
        P("col", "row"),
        P("row"),
        P("row"),
        P("row", "col"),
        P("row", "col"),
        P("col", "row"),
        P(("dp", "row")),
        P(("dp", "col"), "row"),
    )
    out_specs = (
        P(("dp", "col"), "row"),
        P(("dp", "col"), "row"),
        P("row"),
        P("row"),
        P("row", "col"),
        P("row", "col"),
        P("row", "col"),
        P("row", "col"),
        P("col", "row"),
        P("row"),
        P("row"),
        P("row", "col"),
        P("row", "col"),
        P("col", "row"),
    )
    return jax.shard_map(
        per_device, mesh=mesh, in_specs=in_specs, out_specs=out_specs, check_vma=False
    )
```
